256 devices in a mesh: space: 32 (over y, x, core), spin: 2 (over z_hi), cons: 4 (over z_lo).
Axes of the slice: x: 4, y: 4, z: 8 (z_hi: 2, z_lo: 4; z = z_hi * 4 + z_lo), core: 2. Of those that a mesh axis runs over, the one named last changes fastest.
Arguments:
- eigvecs: bfloat16 [2, 2, 256, 61440], P(None, None, None, 'space'), may hold values from -0.0234375 to 0.0234375
- solutions: bfloat16 [2, 2, 4, 256, 61440], P(None, None, 'spin', 'cons', 'space'), may hold values from -6 to 6
- elementals: bfloat16 [8, 2, 256, 256], replicated, may hold values from -0.375 to 0.375
- op_list: int32 [256, 16, 4], P(('space', 'spin', 'cons')), may hold values from 0 to 7, as said below
- live_count: int32 [256], P(('space', 'spin', 'cons')), may hold values from 1 to 16, as said below
Outputs:
- blocks: bfloat16 [2, 4096, 256, 256], P(None, ('space', 'spin', 'cons'))
The draws below stay inside these ranges and needn't reach their ends.
Inputs may be any that keep to these rules, and one draw needn't show every extreme that they name: `op_list`: columns hold an elemental in 0 to 7, two sink spins in 0 to 3 and a sink slice in 0 to 1; slots at or beyond an owner's live count hold arbitrary entries of that kind. `live_count`: some owner has all 16 slots live.
All inputs are finite; a program needn't handle non-finite values.
Results may differ from the reference program's by a relative error of at most 0.0064.
Values may be sent and summed in bfloat16 or wider, within the bound.
A program may use at most 128 MiB of HBM per device.

```python
import jax
import jax.numpy as jnp
from jax import lax

NEV = 256
NT = 2
NELEM = 8
SLOTS = 16
ROWS = 61440
OWNERS = 256


def draw_op_list(key, part):
    keys = jax.random.split(key, 4)
    elem = jax.random.randint(keys[0], (OWNERS, SLOTS), 0, NELEM)
    spin_a = jax.random.randint(keys[1], (OWNERS, SLOTS), 0, 4)
    spin_b = jax.random.randint(keys[2], (OWNERS, SLOTS), 0, 4)
    slice_t = jax.random.randint(keys[3], (OWNERS, SLOTS), 0, NT)
    first = (jnp.arange(OWNERS)[:, None] == 0) & (jnp.arange(SLOTS)[None, :] == 0)
    elem = jnp.where(first, NELEM - 1, elem)
    spin_a = jnp.where(first, 0, spin_a)
    spin_b = jnp.where(first, 3, spin_b)
    return jnp.stack([elem, spin_a, spin_b, slice_t], axis=-1).astype(jnp.int32)


def draw_live_count(key, part):
    keys = jax.random.split(key, 2)
    counts = jax.random.randint(keys[0], (OWNERS,), 1, SLOTS + 1)
    fullest = jax.random.randint(keys[1], (), 0, OWNERS)
    counts = jnp.where(jnp.arange(OWNERS) == fullest, SLOTS, counts)
    return counts.astype(jnp.int32)


def block_levels(rng, extent, cuts, smallest, top_value):
    gain = 1.0
    for position, parts in cuts:
        steps = jax.random.uniform(jax.random.fold_in(jax.random.fold_in(rng, 6), position), (parts,), jnp.float32, smallest / len(cuts), top_value / len(cuts))
        gain = gain * jnp.repeat(jnp.exp(steps), extent[position] // parts).reshape((-1,) + (1,) * (len(extent) - 1 - position))
    return gain


def bell_draw(key, extent, scale, bound, pieces=(), held_as=jnp.bfloat16):
    array = jax.random.normal(key, extent, jnp.float32) * scale
    if len(pieces) > 0:
        array = block_levels(key, extent, pieces, -0.22, 0.18) * array
    return jnp.clip(array, min=-bound, max=bound).astype(held_as)


def setup_inputs(seed: int = 0) -> dict:
    key_list = jax.random.split(jax.random.key(seed), 6)
    return {
        "eigvecs": bell_draw(key_list[0], (2, NT, NEV, ROWS), ROWS ** -0.5, 0.0234375, ((3, 32),)),
        "solutions": bell_draw(key_list[1], (2, NT, 4, NEV, ROWS), 1.0, 6.0, ((2, 2), (3, 4), (4, 32))),
        "elementals": bell_draw(key_list[2], (NELEM, 2, NEV, NEV), NEV ** -0.5, 0.375),
        "op_list": draw_op_list(jax.random.fold_in(key_list[5], 71), 0),
        "live_count": draw_live_count(jax.random.fold_in(key_list[5], 71), 0),
    }


def contract(left, phi, right):
    prod = jnp.einsum("pik,qkj->pqij", phi.astype(jnp.float32), right.astype(jnp.float32))
    mixed = jnp.stack([prod[0, 0] - prod[1, 1], prod[0, 1] + prod[1, 0]]).astype(jnp.bfloat16)
    prod_two = jnp.einsum("pki,qkj->pqij", left.astype(jnp.float32), mixed.astype(jnp.float32))
    return jnp.stack([prod_two[0, 0] + prod_two[1, 1], prod_two[0, 1] - prod_two[1, 0]]) * (NEV ** -0.5)


def reference(eigvecs, solutions, elementals, op_list, live_count):
    def project(slice_t):
        vecs = eigvecs[:, slice_t].astype(jnp.float32)
        sols = solutions[:, slice_t].astype(jnp.float32)
        prod = jnp.einsum("pir,qsjr->pqsij", vecs, sols)
        return jnp.stack([prod[0, 0] + prod[1, 1], prod[0, 1] - prod[1, 0]])

    tau = lax.map(project, jnp.arange(NT)).astype(jnp.bfloat16)
    flat = jnp.transpose(tau, (1, 0, 2, 3, 4)).reshape(2, NT * 4, NEV, NEV)
    items = op_list.reshape(OWNERS * SLOTS, 4)
    live = (jnp.arange(SLOTS)[None, :] < live_count[:, None]).reshape(OWNERS * SLOTS)

    def one_item(packed):
        item, keep = packed
        left = flat[:, item[3] * 4 + item[1]]
        right = flat[:, item[3] * 4 + item[2]]
        result = contract(left, elementals[item[0]], right)
        return jnp.where(keep, result, jnp.zeros_like(result)).astype(jnp.bfloat16)

    results = lax.map(one_item, (items, live))
    return jnp.transpose(results, (1, 0, 2, 3))
```

```python
import jax
import jax.numpy as jnp
from jax import lax
from jax.experimental import pallas as pl
from jax.experimental.pallas import tpu as pltpu
from jax.sharding import PartitionSpec as P

BF16 = jnp.bfloat16
F32 = jnp.float32
NT_DIMS = (((1,), (1,)), ((), ()))
SENDS = ((0, 0, 1), (0, 1, -1), (0, 1, 1), (0, 0, -1), (-1, 0, 1), (1, 1, -1))
LANDED = ((-1, 0), (1, 1), (-1, 1), (1, 0), (2, 0), (2, 1))


def wait_bytes(ref, sem):
    pltpu.make_async_copy(ref, ref, sem).wait()


def gather_kernel(eig, sol, tau, vbuf, sbuf, part, mine, recv, in_sem, rs_send, rs_recv, z_send, z_recv,
                  ring_send, ring_recv, chip_send, chip_recv):
    sp = lax.axis_index("space")
    z_hi = lax.axis_index("spin")
    z_lo = lax.axis_index("cons")
    core = lax.rem(sp, 2)
    chip = lax.div(sp, 2)
    x = lax.rem(chip, 4)
    y = lax.div(chip, 4)
    z = z_hi * 4 + z_lo
    re_im = lax.div(y, 2)
    half = lax.rem(y, 2)

    loads = []
    for t in range(2):
        loads.append((
            pltpu.make_async_copy(eig.at[:, t], vbuf.at[t], in_sem.at[2 * t]),
            pltpu.make_async_copy(sol.at[:, t], sbuf.at[t], in_sem.at[2 * t + 1]),
        ))
        for c in loads[t]:
            c.start()

    def at_space(d):
        return {"space": d}

    def at_z(d):
        return {"spin": lax.div(d, 4), "cons": lax.rem(d, 4)}

    barrier = pltpu.get_barrier_semaphore()

    def greet_plane(r, carry):
        pl.semaphore_signal(barrier, inc=1, device_id=at_space(lax.rem(sp + r, 32)))
        return carry

    def greet_z(r, carry):
        pl.semaphore_signal(barrier, inc=1, device_id=at_z(lax.rem(z + r, 8)))
        return carry

    lax.fori_loop(1, 32, greet_plane, 0)
    lax.fori_loop(1, 8, greet_z, 0)

    for t in range(2):
        for c in loads[t]:
            c.wait()
        v = vbuf[t].reshape(512, 1920)
        s = sbuf[t].reshape(256, 1920)
        prod = lax.dot_general(s, v, NT_DIMS, preferred_element_type=F32)
        re = prod[:128, :256] + prod[128:, 256:]
        im = prod[128:, :256] - prod[:128, 256:]
        re = re.reshape(8, 16, 256)
        im = im.reshape(8, 16, 256)
        mine[t, 0:8] = re
        mine[t, 8:16] = im
        part[t, 0:8] = re.astype(BF16)
        part[t, 8:16] = im.astype(BF16)
        if t == 0:
            pl.semaphore_wait(barrier, 38)

        def send(q, carry, t=t):
            p = lax.rem(chip + q, 16)
            d = 2 * p + t
            slot = lax.rem(sp - d + 32, 32) - 1

            @pl.when(d != sp)
            def _():
                pltpu.make_async_remote_copy(
                    src_ref=part.at[t, p], dst_ref=recv.at[slot], send_sem=rs_send, recv_sem=rs_recv,
                    device_id=at_space(d)).start()

            return carry

        lax.fori_loop(0, 16, send, 0)

    wait_bytes(recv, rs_recv)
    total = mine[core, chip]
    for k in range(31):
        total = total + recv[k].astype(F32)
    own = tau.at[core, re_im, z_hi, half, z_lo, x]
    own[...] = total.astype(BF16)

    def send_z(r, carry):
        pltpu.make_async_remote_copy(
            src_ref=own, dst_ref=own, send_sem=z_send, recv_sem=z_recv,
            device_id=at_z(lax.rem(z + r, 8))).start()
        return carry

    lax.fori_loop(1, 8, send_z, 0)

    def x_peer(k):
        return (y * 4 + lax.rem(x + k + 4, 4)) * 2 + core

    def y_peer(k):
        return (lax.rem(y + k + 4, 4) * 4 + x) * 2 + core

    def block_1x(k, h):
        return tau.at[core, re_im, 0, half, pl.ds(2 * h, 2), lax.rem(x + k + 4, 4)]

    def block_1y(k, h):
        yy = lax.rem(y + k + 4, 4)
        return tau.at[core, lax.div(yy, 2), 1, lax.rem(yy, 2), pl.ds(2 * h, 2), x]

    def block_2y(k, h):
        yy = lax.rem(y + k + 4, 4)
        return tau.at[core, lax.div(yy, 2), 0, lax.rem(yy, 2), pl.ds(2 * h, 2)]

    def block_2x(k, h):
        return tau.at[core, :, 1, :, pl.ds(2 * h, 2), lax.rem(x + k + 4, 4)]

    class Ring:
        def __init__(self, i, block, peer):
            self.i, self.block, self.peer = i, block, peer

        def copy(self, n, ref, step):
            return pltpu.make_async_remote_copy(
                src_ref=ref, dst_ref=ref, send_sem=ring_send.at[self.i, n], recv_sem=ring_recv.at[self.i, n],
                device_id=at_space(self.peer(step)))

        def send(self, n):
            k, h, step = SENDS[n]
            return self.copy(n, self.block(k, h), step)

        def landed(self, n):
            return self.block(*LANDED[n])

        def start(self):
            for n in range(4):
                self.send(n).start()

        def wait(self, n):
            wait_bytes(self.landed(n), ring_recv.at[self.i, n])

        def forward(self):
            self.wait(0)
            self.send(4).start()
            self.wait(1)
            self.send(5).start()

        def drain(self):
            for n in range(6):
                self.send(n).wait_send()

    ring_1x = Ring(0, block_1x, x_peer)
    ring_1y = Ring(1, block_1y, y_peer)
    ring_2y = Ring(2, block_2y, y_peer)
    ring_2x = Ring(3, block_2x, x_peer)

    partner = sp + 1 - 2 * core

    def chip_copy(n, ref):
        return pltpu.make_async_remote_copy(
            src_ref=ref, dst_ref=ref, send_sem=chip_send.at[n], recv_sem=chip_recv.at[n],
            device_id=at_space(partner))

    wait_bytes(recv.at[pl.ds(0, 7)], z_recv)
    ring_1x.start()
    ring_1y.start()
    ring_1x.forward()
    ring_1y.forward()
    for n in range(2, 6):
        ring_1x.wait(n)
    ring_2y.start()
    for n in range(2, 6):
        ring_1y.wait(n)
    ring_2x.start()
    shares = [block_2y(0, 0), block_2y(0, 1), block_2x(0, 0), block_2x(0, 1)]
    for n in range(4):
        chip_copy(n, shares[n]).start()
    ring_2y.forward()
    ring_2x.forward()
    for n in range(6):
        for ring in (ring_2y, ring_2x):
            if n >= 2:
                ring.wait(n)
            shares.append(ring.landed(n))
            chip_copy(len(shares) - 1, shares[-1]).start()
    for n in range(len(shares)):
        wait_bytes(shares[n], chip_recv.at[n])
    wait_bytes(recv, rs_send)
    wait_bytes(recv.at[pl.ds(0, 7)], z_send)
    for ring in (ring_1x, ring_1y, ring_2y, ring_2x):
        ring.drain()
    for n in range(len(shares)):
        chip_copy(n, shares[n]).wait_send()


def gather_tau(eigvecs, solutions):
    return pl.pallas_call(
        gather_kernel,
        out_shape=pltpu.VMEM((2, 2, 2, 2, 4, 4, 16, 256), BF16),
        in_specs=[pl.BlockSpec(memory_space=pltpu.HBM)] * 2,
        out_specs=pl.BlockSpec(memory_space=pltpu.VMEM),
        scratch_shapes=[
            pltpu.VMEM((2, 2, 256, 1920), BF16),
            pltpu.VMEM((2, 2, 2, 64, 1920), BF16),
            pltpu.VMEM((2, 16, 16, 256), BF16),
            pltpu.VMEM((2, 16, 16, 256), F32),
            pltpu.VMEM((31, 16, 256), BF16),
            pltpu.SemaphoreType.DMA((4,)),
            pltpu.SemaphoreType.DMA,
            pltpu.SemaphoreType.DMA,
            pltpu.SemaphoreType.DMA,
            pltpu.SemaphoreType.DMA,
            pltpu.SemaphoreType.DMA((4, 6)),
            pltpu.SemaphoreType.DMA((4, 6)),
            pltpu.SemaphoreType.DMA((16,)),
            pltpu.SemaphoreType.DMA((16,)),
        ],
        compiler_params=pltpu.CompilerParams(collective_id=0, has_side_effects=True, vmem_limit_bytes=24 << 20),
        name="gather_tau",
    )(eigvecs, solutions)


def blocks_kernel(items, count, tau, elem, out, buf, sem):
    n_slots = 16

    def put(k):
        return pltpu.make_async_copy(buf.at[lax.rem(k, 4)], out.at[:, k], sem.at[lax.rem(k, 4)])

    def one(k, carry):
        e = items[k, 0]
        a = items[k, 1]
        b = items[k, 2]
        t = items[k, 3]
        slot = lax.rem(k, 4)

        @pl.when(k >= 4)
        def _():
            put(k - 4).wait()

        @pl.when(k < count[0])
        def _():
            phi_re, phi_im = elem[e, 0], elem[e, 1]
            phi = jnp.concatenate([
                jnp.concatenate([phi_re, -phi_im], axis=1),
                jnp.concatenate([phi_im, phi_re], axis=1)], axis=0)
            right = jnp.concatenate([tau[t, 0, b], tau[t, 1, b]], axis=1)
            mixed = lax.dot_general(phi, right, NT_DIMS, preferred_element_type=F32).astype(BF16)
            left_re, left_im = tau[t, 0, a], tau[t, 1, a]
            left = jnp.concatenate([
                jnp.concatenate([left_re, left_im], axis=1),
                jnp.concatenate([-left_im, left_re], axis=1)], axis=0)
            res = jnp.dot(left, mixed, preferred_element_type=F32) * (256.0 ** -0.5)
            buf[slot] = res.astype(BF16).reshape(2, 256, 256)

        @pl.when(k >= count[0])
        def _():
            buf[slot] = jnp.zeros((2, 256, 256), BF16)

        put(k).start()
        return carry

    lax.fori_loop(0, n_slots, one, 0)
    for k in range(n_slots - 4, n_slots):
        put(k).wait()


def make_blocks(items, count, tau, elementals):
    return pl.pallas_call(
        blocks_kernel,
        out_shape=jax.ShapeDtypeStruct((2, 16, 256, 256), BF16),
        in_specs=[
            pl.BlockSpec(memory_space=pltpu.SMEM),
            pl.BlockSpec(memory_space=pltpu.SMEM),
            pl.BlockSpec(memory_space=pltpu.VMEM),
            pl.BlockSpec(memory_space=pltpu.VMEM),
        ],
        out_specs=pl.BlockSpec(memory_space=pl.ANY),
        scratch_shapes=[pltpu.VMEM((4, 2, 256, 256), BF16), pltpu.SemaphoreType.DMA((4,))],
        compiler_params=pltpu.CompilerParams(vmem_limit_bytes=24 << 20),
        name="make_blocks",
    )(items, count, tau, elementals)


def body(eigvecs, solutions, elementals, op_list, live_count):
    tau = gather_tau(eigvecs, solutions).reshape(2, 2, 4, 256, 256)
    return make_blocks(op_list[0], live_count, tau, elementals)


def solution(mesh):
    return jax.shard_map(
        body,
        mesh=mesh,
        in_specs=(
            P(None, None, None, "space"),
            P(None, None, "spin", "cons", "space"),
            P(),
            P(("space", "spin", "cons"), None, None),
            P(("space", "spin", "cons")),
        ),
        out_specs=P(None, ("space", "spin", "cons"), None, None),
        check_vma=False,
    )
```

```python
import jax
import jax.numpy as jnp
from jax import lax
from jax.experimental import pallas as pl
from jax.experimental.pallas import tpu as pltpu
from jax.sharding import PartitionSpec as P

BF16 = jnp.bfloat16
F32 = jnp.float32
NT_DIMS = (((1,), (1,)), ((), ()))
OTHERS = sorted(
    [(dx, dy) for dx in range(4) for dy in range(4) if dx or dy],
    key=lambda d: -(min(d[0], 4 - d[0]) + min(d[1], 4 - d[1])))
PLANES = (4, 3, 5, 2, 6, 1, 7)
LINES = (0, 1, 3, 2)


def wait_bytes(ref, sem):
    pltpu.make_async_copy(ref, ref, sem).wait()


def gather_kernel(eig, sol, tau, vbuf, sbuf, give, take, mine, part, recv, in_sem, pair_send, pair_recv,
                  sum_send, sum_recv, z_send, z_recv, one_send, one_recv, two_send, pass_send, two_recv,
                  chip_send, chip_recv):
    sp = lax.axis_index("space")
    z_hi = lax.axis_index("spin")
    z_lo = lax.axis_index("cons")
    core = lax.rem(sp, 2)
    chip = lax.div(sp, 2)
    x = lax.rem(chip, 4)
    y = lax.div(chip, 4)
    z = z_hi * 4 + z_lo

    def load(n):
        t = 1 - core if n == 0 else core
        return [
            pltpu.make_async_copy(src.at[p, t], dst.at[n, p], in_sem.at[n, p, i])
            for p in range(2) for i, (src, dst) in enumerate(((eig, vbuf), (sol, sbuf)))]

    loads = [load(0), load(1)]
    for c in loads[0] + loads[1]:
        c.start()

    def at_chip(dx, dy):
        return {"space": (lax.rem(y + dy, 4) * 4 + lax.rem(x + dx, 4)) * 2 + core}

    def at_plane(r):
        d = lax.rem(z + r, 8)
        return {"spin": lax.div(d, 4), "cons": lax.rem(d, 4)}

    partner = {"space": sp + 1 - 2 * core}
    everyone = [partner] + [at_chip(*d) for d in OTHERS] + [at_plane(r) for r in PLANES]
    barrier = pltpu.get_barrier_semaphore()
    for d in everyone:
        pl.semaphore_signal(barrier, inc=1, device_id=d)

    def remote(src, dst, send, recv, device):
        return pltpu.make_async_remote_copy(src_ref=src, dst_ref=dst, send_sem=send, recv_sem=recv, device_id=device)

    def partial(n):
        for c in loads[n]:
            c.wait()
        v = vbuf[n].reshape(512, 1920)
        s = sbuf[n].reshape(256, 1920)
        prod = lax.dot_general(s, v, NT_DIMS, preferred_element_type=F32)
        re = prod[:128, :256] + prod[128:, 256:]
        im = prod[128:, :256] - prod[:128, 256:]
        return re.reshape(8, 16, 256), im.reshape(8, 16, 256)

    give[0:8], give[8:16] = partial(0)
    pl.semaphore_wait(barrier, len(everyone))
    remote(give, take, pair_send, pair_recv, partner).start()
    mine[0:8], mine[8:16] = partial(1)
    wait_bytes(take, pair_recv)
    both = mine[...] + take[...]
    mine[...] = both
    part[...] = both.astype(BF16)
    for n, (dx, dy) in enumerate(OTHERS):
        remote(part.at[lax.rem(y + dy, 4) * 4 + lax.rem(x + dx, 4)], recv.at[n], sum_send, sum_recv,
               at_chip(dx, dy)).start()
    wait_bytes(recv, sum_recv)
    total = mine[chip]
    for n in range(15):
        total = total + recv[n].astype(F32)

    def piece(r, dx=0, dy=0):
        zz = lax.rem(z + r, 8)
        yy = lax.rem(y + dy, 4)
        return tau.at[core, lax.div(yy, 2), lax.div(zz, 4), lax.rem(yy, 2), lax.rem(zz, 4), lax.rem(x + dx, 4)]

    own = piece(0)
    own[...] = total.astype(BF16)
    for r in PLANES:
        remote(own, own, z_send, z_recv.at[r - 1], at_plane(r)).start()

    def spread(r):
        hi = lax.div(lax.rem(z + r, 8), 4)
        for k in (2, 1, 3):
            xx = lax.rem(x + k * (1 - hi), 4)
            yy = lax.rem(y + k * hi, 4)
            remote(piece(r), piece(r), one_send, one_recv.at[hi, k - 1],
                   {"space": (yy * 4 + xx) * 2 + core}).start()

    spread(0)
    for r in reversed(PLANES):
        wait_bytes(piece(r), z_recv.at[8 - r - 1])
        spread(r)

    def line(hi, k, step):
        dx, dy = (k, step) if hi == 0 else (step, k)
        yy = lax.rem(y + dy, 4)
        return tau.at[core, lax.div(yy, 2), hi, lax.rem(yy, 2), :, lax.rem(x + dx, 4)]

    def ring_peer(hi, step):
        return at_chip(0, step) if hi == 0 else at_chip(step, 0)

    def two(hi, k, n, step, send, to):
        ref = line(hi, k, step)
        return remote(ref, ref, send, two_recv.at[hi, k, n], ring_peer(hi, to))

    def share(ref):
        remote(ref, ref, chip_send, chip_recv, partner).start()

    def begin(hi, k):
        if k:
            wait_bytes(line(hi, k, 0), one_recv.at[hi, 4 - k - 1])
        two(hi, k, 0, 0, two_send, 1).start()
        two(hi, k, 1, 0, two_send, 3).start()
        share(line(hi, k, 0))

    def landed(hi, k, n):
        step = (3, 1, 2)[n]
        wait_bytes(line(hi, k, step), two_recv.at[hi, k, n])
        if n == 0 and k in (0, 2):
            two(hi, k, 2, 3, pass_send, 1).start()
        if n == 1 and k in (1, 3):
            two(hi, k, 2, 1, pass_send, 3).start()
        share(line(hi, k, step))

    for k in LINES:
        for hi in range(2):
            begin(hi, k)
    for k in LINES:
        for n in range(2):
            for hi in range(2):
                landed(hi, k, n)
    for k in LINES:
        for hi in range(2):
            landed(hi, k, 2)
    wait_bytes(tau.at[1 - core], chip_recv)
    wait_bytes(give, pair_send)
    wait_bytes(recv, sum_send)
    wait_bytes(recv.at[pl.ds(0, 7)], z_send)
    wait_bytes(give.at[pl.ds(0, 12)], one_send)
    wait_bytes(tau.at[core, 0], two_send)
    wait_bytes(tau.at[core, 0, 0], pass_send)
    wait_bytes(tau.at[core], chip_send)


def gather_tau(eigvecs, solutions):
    dma = pltpu.SemaphoreType.DMA
    return pl.pallas_call(
        gather_kernel,
        out_shape=pltpu.VMEM((2, 2, 2, 2, 4, 4, 16, 256), BF16),
        in_specs=[pl.BlockSpec(memory_space=pltpu.HBM)] * 2,
        out_specs=pl.BlockSpec(memory_space=pltpu.VMEM),
        scratch_shapes=[
            pltpu.VMEM((2, 2, 256, 1920), BF16),
            pltpu.VMEM((2, 2, 2, 64, 1920), BF16),
            pltpu.VMEM((16, 16, 256), F32),
            pltpu.VMEM((16, 16, 256), F32),
            pltpu.VMEM((16, 16, 256), F32),
            pltpu.VMEM((16, 16, 256), BF16),
            pltpu.VMEM((15, 16, 256), BF16),
            dma((2, 2, 2)),
            dma, dma,
            dma, dma,
            dma, dma((7,)),
            dma, dma((2, 3)),
            dma, dma, dma((2, 4, 3)),
            dma, dma,
        ],
        compiler_params=pltpu.CompilerParams(collective_id=0, has_side_effects=True, vmem_limit_bytes=24 << 20),
        name="gather_tau",
    )(pltpu.with_memory_space_constraint(eigvecs, pltpu.HBM), pltpu.with_memory_space_constraint(solutions, pltpu.HBM))


def blocks_kernel(items, count, tau, elem, out, buf, sem):
    n_slots = 16

    def put(k):
        return pltpu.make_async_copy(buf.at[lax.rem(k, 4)], out.at[:, k], sem.at[lax.rem(k, 4)])

    def mix(k):
        e = items[0, k]
        b = items[2, k]
        t = items[3, k]
        phi_re, phi_im = elem[e, 0], elem[e, 1]
        phi = jnp.concatenate([
            jnp.concatenate([phi_re, -phi_im], axis=1),
            jnp.concatenate([phi_im, phi_re], axis=1)], axis=0)
        right = jnp.concatenate([tau[t, 0, b], tau[t, 1, b]], axis=1)
        return lax.dot_general(phi, right, NT_DIMS, preferred_element_type=F32).astype(BF16)

    def finish(k, mixed):
        a = items[1, k]
        t = items[3, k]
        left_re, left_im = tau[t, 0, a], tau[t, 1, a]
        left = jnp.concatenate([
            jnp.concatenate([left_re, left_im], axis=1),
            jnp.concatenate([-left_im, left_re], axis=1)], axis=0)
        res = jnp.dot(left, mixed, preferred_element_type=F32) * (256.0 ** -0.5)
        return jnp.where(k < count[0], res, 0.0).astype(BF16).reshape(2, 256, 256)

    def two(n, carry):
        k = 2 * n

        @pl.when(n >= 2)
        def _():
            put(k - 4).wait()
            put(k - 3).wait()

        @pl.when(k < count[0])
        def _():
            mixed = [mix(k), mix(k + 1)]
            for i in range(2):
                buf[lax.rem(k + i, 4)] = finish(k + i, mixed[i])

        @pl.when(k >= count[0])
        def _():
            for i in range(2):
                buf[lax.rem(k + i, 4)] = jnp.zeros((2, 256, 256), BF16)

        put(k).start()
        put(k + 1).start()
        return carry

    lax.fori_loop(0, n_slots // 2, two, 0)
    for k in range(n_slots - 4, n_slots):
        put(k).wait()


def make_blocks(items, count, tau, elementals):
    return pl.pallas_call(
        blocks_kernel,
        out_shape=jax.ShapeDtypeStruct((2, 16, 256, 256), BF16),
        in_specs=[
            pl.BlockSpec(memory_space=pltpu.SMEM),
            pl.BlockSpec(memory_space=pltpu.SMEM),
            pl.BlockSpec(memory_space=pltpu.VMEM),
            pl.BlockSpec(memory_space=pltpu.VMEM),
        ],
        out_specs=pl.BlockSpec(memory_space=pl.ANY),
        scratch_shapes=[pltpu.VMEM((4, 2, 256, 256), BF16), pltpu.SemaphoreType.DMA((4,))],
        compiler_params=pltpu.CompilerParams(vmem_limit_bytes=24 << 20),
        name="make_blocks",
    )(items, count, tau, elementals)


def body(eigvecs, solutions, elementals, op_list, live_count):
    tau = gather_tau(eigvecs, solutions).reshape(2, 2, 4, 256, 256)
    return make_blocks(op_list[0].T, live_count, tau, elementals)


def solution(mesh):
    return jax.shard_map(
        body,
        mesh=mesh,
        in_specs=(
            P(None, None, None, "space"),
            P(None, None, "spin", "cons", "space"),
            P(),
            P(("space", "spin", "cons"), None, None),
            P(("space", "spin", "cons")),
        ),
        out_specs=P(None, ("space", "spin", "cons"), None, None),
        check_vma=False,
    )
```
